512 devices in a mesh: ctx: 64 (over x, y_lo, z), fsdp: 8 (over y_hi, core).
Axes of the slice: x: 4, y: 8 (y_hi: 4, y_lo: 2; y = y_hi * 2 + y_lo), z: 8, core: 2. Of those that a mesh axis runs over, the one named last changes fastest.
Arguments:
- queries: bfloat16 [2, 16384, 2048], P(None, 'ctx', 'fsdp'), may hold values from -5.5 to 5.5
- keys_values: bfloat16 [2, 2, 16384, 2048], P(None, None, 'ctx', 'fsdp'), may hold values from -5.5 to 5.5
- block_mask: int32 [256, 32], P('ctx'), may hold values 0 or 1
- out_weight: bfloat16 [2048, 4096], P('fsdp'), may hold values from -3 to 3
Outputs:
- mixed: bfloat16 [2, 16384, 4096], P(None, 'ctx', 'fsdp')
The draws below stay inside these ranges and needn't reach their ends.
All inputs are finite; a program needn't handle non-finite values. No bound on the sum of `block_mask` on one device may be relied on, other than what follows from the above.
Results may differ from the reference program's by a relative error of at most 0.0058.
Values may be sent and summed in bfloat16 or wider, within the bound.
A program may use at most 64 MiB of HBM per device.

```python
import math
import jax
import jax.numpy as jnp
from jax import lax

D = 4096
HD = 128
BLK = 64
WINB = 32
TOK_DEV = 256
HH = 2048
LEN = 16384
NBLOCKS = 256
N_CTX = 64


def drawn_rows(key, salt, shape):
    base = jax.random.normal(jax.random.fold_in(key, salt), shape, jnp.float32)
    return jnp.clip(base, -5.5, 5.5)


def draw_queries(key, part):
    return drawn_rows(key, 11, (2, LEN, HH)).astype(jnp.bfloat16)


def draw_keys_values(key, part):
    keys = drawn_rows(key, 21, (2, LEN, HH))
    values = jax.random.normal(jax.random.fold_in(key, 31), (2, LEN, HH), jnp.float32)
    values = jnp.clip(values, -5.5, 5.5)
    return jnp.stack([keys, values]).astype(jnp.bfloat16)


def place_ends(drawn, key, smallest, largest):
    extent = drawn.shape
    place = [jax.random.randint(jax.random.fold_in(key, axis), (), 0, extent[axis]) for axis in range(len(extent))]
    drawn = drawn.at[tuple(place)].set(smallest)
    longest = extent.index(max(extent))
    place[longest] = (place[longest] + 1) % extent[longest]
    return drawn.at[tuple(place)].set(largest)


def shard_levels(own_key, extent, cuts, low, top_value):
    def one(position, shards_of):
        steps = jax.random.uniform(jax.random.fold_in(jax.random.fold_in(own_key, 6), position), (shards_of,), jnp.float32, low / len(cuts), top_value / len(cuts))
        return jnp.repeat(jnp.exp(steps), extent[position] // shards_of).reshape((-1,) + (1,) * (len(extent) - position - 1))

    level = one(*cuts[0])
    for cut in cuts[1:]:
        level = level * one(*cut)
    return level


def normal_values(rng, extent, spread, bound, cuts=(), kind=jnp.bfloat16):
    factor_of = shard_levels(rng, extent, cuts, -0.22, 0.18) if cuts else 1.0
    values = jax.random.normal(rng, extent, jnp.float32) * spread * factor_of
    return jnp.minimum(jnp.maximum(values, -bound), bound).astype(kind)


def setup_inputs(seed: int = 0) -> dict:
    key_of = jax.random.split(jax.random.key(seed), 5)
    return {
        "queries": draw_queries(jax.random.fold_in(key_of[4], 71), 0),
        "keys_values": draw_keys_values(jax.random.fold_in(key_of[4], 71), 0),
        "block_mask": place_ends((jax.random.randint(key_of[2], (NBLOCKS, WINB), 0, 2) < 1).astype(jnp.int32), jax.random.fold_in(key_of[2], 1), 0, 1),
        "out_weight": normal_values(key_of[3], (HH, D), (max(1, HH // 512)) ** -0.5, 3.0, ((0, 8),)),
    }


def block_rules(first_block, query_count, key_start, key_count, mask_rows):
    query_blocks = first_block + jnp.arange(query_count, dtype=jnp.int32)
    key_blocks = key_start + jnp.arange(key_count, dtype=jnp.int32)
    block_gap = query_blocks[:, None] - key_blocks[None, :]
    present = key_blocks[None, :] >= 0
    clean_ok = (block_gap >= 0) & (block_gap < WINB) & present
    offsets = jnp.arange(WINB, dtype=jnp.int32)
    picked = ((block_gap - 1)[:, :, None] == offsets[None, None, :]) & (mask_rows[:, None, :] == 1)
    noisy_ok = jnp.any(picked, axis=2) & present
    own_block = query_blocks[:, None] == query_blocks[None, :]

    def widen(table):
        return jnp.repeat(jnp.repeat(table, BLK, axis=0), BLK, axis=1)
    return (widen(clean_ok), widen(noisy_ok), widen(own_block))

def attend(query, keys, values, allowed):
    count, width = query.shape
    heads = width // HD
    query_three = query.astype(jnp.float32).reshape(count, heads, HD)
    key_three = keys.astype(jnp.float32).reshape(-1, heads, HD)
    value_three = values.astype(jnp.float32).reshape(-1, heads, HD)
    scores = jnp.einsum('qhd,khd->hqk', query_three, key_three) * (1.0 / math.sqrt(HD))
    scores = jnp.where(allowed[None], scores, jnp.float32(-1e+30))
    top = lax.optimization_barrier(jnp.max(scores, axis=-1, keepdims=True))
    expo = jnp.exp(scores - top)
    weights = (expo / lax.optimization_barrier(jnp.sum(expo, axis=-1, keepdims=True))).astype(jnp.bfloat16)
    result = jnp.einsum('hqk,khd->qhd', weights.astype(jnp.float32), value_three)
    return result.reshape(count, width).astype(jnp.bfloat16)

def reference(queries, keys_values, block_mask, out_weight):
    span = WINB * BLK
    blocks_dev = TOK_DEV // BLK
    clean_pair = jnp.pad(keys_values[:, 0], ((0, 0), (span, 0), (0, 0)))
    noisy_pair = keys_values[:, 1]

    def group_step(index):
        start = index * TOK_DEV
        zero = jnp.int32(0)
        window = lax.dynamic_slice(clean_pair, (zero, start, zero), (2, span + TOK_DEV, HH))
        own_query = lax.dynamic_slice(queries, (zero, start, zero), (2, TOK_DEV, HH))
        own_pair = lax.dynamic_slice(noisy_pair, (zero, start, zero), (2, TOK_DEV, HH))
        mask_rows = lax.dynamic_slice(block_mask, (index * blocks_dev, zero), (blocks_dev, WINB))
        first_block = index * blocks_dev
        clean_ok, noisy_ok, own_ok = block_rules(first_block, blocks_dev, first_block - WINB, blocks_dev + WINB, mask_rows)
        clean_out = attend(own_query[0], window[0], window[1], clean_ok)
        noisy_keys = jnp.concatenate([window[0], own_pair[0]], axis=0)
        noisy_values = jnp.concatenate([window[1], own_pair[1]], axis=0)
        noisy_allowed = jnp.concatenate([noisy_ok, own_ok], axis=1)
        noisy_out = attend(own_query[1], noisy_keys, noisy_values, noisy_allowed)
        return jnp.stack([clean_out, noisy_out])
    pieces = lax.map(group_step, jnp.arange(N_CTX, dtype=jnp.int32))
    attended = jnp.transpose(pieces, (1, 0, 2, 3)).reshape(2 * LEN, HH)
    mixed = jnp.dot(attended, out_weight, preferred_element_type=jnp.float32)
    return mixed.astype(jnp.bfloat16).reshape(2, LEN, D)
```

```python
import functools
import math

import jax
import jax.numpy as jnp
from jax import lax
from jax.experimental import pallas as pl
from jax.experimental.pallas import tpu as pltpu
from jax.sharding import PartitionSpec as P

HD = 128
BLK = 64
WINB = 32
NX, NL, NZ, NH, NC = 4, 2, 8, 4, 2
NCTX = NX * NL * NZ
ROW = NZ
TOK = 256
BLOCKS = TOK // BLK
HEADS = 2
FEAT = 512
NEG = -1e30
EXP_SCALE = math.log2(math.e) / math.sqrt(HD)


def mod(value, size):
    return lax.rem(value + 2 * size, size)


def kernel(
    mask_ref, q_hbm, kv_hbm, w_hbm, out_ref,
    qbuf, kvbuf, win, bias, top, acc, att, panel, total,
    local_sem, kv_send, kv_recv, ag_send, ag_recv, sib_send, sib_recv,
    wy_send, wy_recv, ws_send, ws_recv, wx_send, wx_recv,
):
    ctx = lax.axis_index("ctx")
    fsdp = lax.axis_index("fsdp")
    x = ctx // (NL * NZ)
    low = lax.rem(ctx // NZ, NL)
    z = lax.rem(ctx, NZ)
    high = fsdp // NC
    core = lax.rem(fsdp, NC)

    def along(by):
        return (mod(ctx + by, NCTX), fsdp)

    def at_high(h, l, c):
        return ((x * NL + l) * NZ + z, h * NC + c)

    def at_x(by):
        return (mod(x + by, NX) * (NL * NZ) + lax.rem(ctx, NL * NZ), fsdp)

    h_up, h_down, h_far = mod(high + 1, NH), mod(high - 1, NH), mod(high + 2, NH)
    sibling = (ctx, high * NC + (1 - core))

    load_kv = pltpu.make_async_copy(kv_hbm, kvbuf, local_sem.at[0])
    load_q = pltpu.make_async_copy(q_hbm, qbuf, local_sem.at[1])
    load_w = pltpu.make_async_copy(
        w_hbm.at[:, :, :, pl.ds(pl.multiple_of(fsdp * FEAT, FEAT), FEAT)],
        panel.at[0, :, core],
        local_sem.at[2],
    )
    load_kv.start()
    load_q.start()
    load_w.start()

    barrier = pltpu.get_barrier_semaphore()
    sources = [along(-1), along(1), along(-ROW)]
    sources += [at_high(h_up, low, core), at_high(h_down, low, core), sibling]
    for c in range(NC):
        sources += [at_high(h_up, 0, c), at_high(h_down, 1, c), at_high(h_far, 1 - low, c)]
    sources += [at_x(1), at_x(-1)]
    for device in sources:
        pl.semaphore_signal(barrier, inc=1, device_id=device, device_id_type=pl.DeviceIdType.MESH)
    pl.semaphore_wait(barrier, len(sources))

    def remote(src, dst, send, recv, device):
        return pltpu.make_async_remote_copy(
            src_ref=src, dst_ref=dst, send_sem=send, recv_sem=recv,
            device_id=device, device_id_type=pl.DeviceIdType.MESH,
        )

    def own(hd, kv):
        return kvbuf.at[kv, 0, :, hd * HD:(hd + 1) * HD]

    def kv_copy(hd, slot, kv):
        forward = slot < 4 or (slot == 4 and kv == 0)
        if forward:
            src = own(hd, kv) if slot == 1 else win.at[hd, slot - 2, kv]
            device = along(1)
        elif slot == 8:
            src, device = own(hd, kv), along(ROW)
        else:
            src, device = win.at[hd, slot, kv], along(-1)
        return remote(src, win.at[hd, slot - 1, kv], kv_send.at[hd, slot - 1, kv],
                      kv_recv.at[hd, slot - 1, kv], device)

    def start_kv(hd):
        for kv in range(2):
            kv_copy(hd, 1, kv).start()
            kv_copy(hd, 8, kv).start()

    load_kv.wait()
    start_kv(0)

    half, part = x // 2, lax.rem(x, 2)
    sign = 2 * low - 1
    w_targets = [
        (mod(high + sign, NH), 0, mod(-sign, NH)),
        (mod(high + sign, NH), 1, mod(-sign, NH)),
        (h_far, 1 - low, 2),
    ]
    w_copies = []
    for n, (h, l, k) in enumerate(w_targets):
        for c in range(NC):
            cols = pl.ds(pl.multiple_of((h * NC + c) * FEAT, FEAT), FEAT)
            w_copies.append(remote(
                w_hbm.at[half, part, :, cols], panel.at[k, half, core, part],
                wy_send.at[n, c], wy_recv, at_high(h, l, c),
            ))
    other = high * NC + (1 - core)
    w_sib = remote(
        w_hbm.at[:, :, :, pl.ds(pl.multiple_of(other * FEAT, FEAT), FEAT)],
        panel.at[0, :, core], ws_send, ws_recv, sibling,
    )
    for copy in w_copies:
        copy.start()
    w_sib.start()

    def w_quarter(by):
        xx = mod(x + by, NX)
        return panel.at[1:4, xx // 2, :, lax.rem(xx, 2)]

    def w_half(by, c):
        xx = mod(x + by, NX)
        return panel.at[1:4, xx // 2, c, lax.rem(xx, 2)]

    def await_bytes(ref, sem):
        pltpu.make_async_copy(ref, ref, sem).wait()

    wx_copies = [
        remote(w_quarter(0), w_quarter(0), wx_send.at[0], wx_recv.at[0], at_x(1)),
        remote(w_quarter(0), w_quarter(0), wx_send.at[1], wx_recv.at[1], at_x(-1)),
        remote(w_half(-1, 0), w_half(-1, 0), wx_send.at[2], wx_recv.at[2], at_x(1)),
        remote(w_half(1, 1), w_half(1, 1), wx_send.at[3], wx_recv.at[3], at_x(-1)),
    ]

    def w_stage_1():
        await_bytes(w_quarter(0), wy_recv)
        wx_copies[0].start()
        wx_copies[1].start()

    def w_stage_2():
        await_bytes(w_quarter(-1), wx_recv.at[0])
        wx_copies[2].start()
        await_bytes(w_quarter(1), wx_recv.at[1])
        wx_copies[3].start()

    lane_block = lax.broadcasted_iota(jnp.int32, (8, TOK), 1) // BLK
    for slot in range(9):
        here = ctx >= slot
        for a in range(BLOCKS):
            clean = jnp.zeros((8, TOK), jnp.int32)
            noisy = jnp.zeros((8, TOK), jnp.int32)
            for b in range(BLOCKS):
                gap = 4 * slot + a - b
                is_b = lane_block == b
                if 0 <= gap < WINB:
                    clean = jnp.where(is_b, 1, clean)
                if 1 <= gap <= WINB:
                    noisy = jnp.where(is_b, mask_ref[a, gap - 1], noisy)
            present = jnp.where(here, 1, 0)
            bias[0, slot, a] = jnp.where(clean * present == 1, 0.0, NEG)
            bias[1, slot, a] = jnp.where(noisy * present == 1, 0.0, NEG)
    for a in range(BLOCKS):
        bias[1, 9, a] = jnp.where(lane_block == a, 0.0, NEG)

    ones = jnp.ones((TOK, HD), jnp.bfloat16)

    def attend(hd, copy, chunks, first):
        q = qbuf[copy, :, hd * HD:(hd + 1) * HD]
        scores = []
        for keys, _, slot in chunks:
            s = lax.dot_general(
                q, keys, (((1,), (1,)), ((), ())), preferred_element_type=jnp.float32
            )
            s = s.reshape(BLOCKS, BLK // 8, 8, TOK) + bias[copy, slot][:, None]
            scores.append(s.reshape(TOK, TOK))
        best = scores[0]
        for s in scores[1:]:
            best = jnp.maximum(best, s)
        best = jnp.max(best, axis=1, keepdims=True)
        if first:
            new_top = jnp.broadcast_to(best, (TOK, HD))
        else:
            old_top = top[copy]
            new_top = jnp.maximum(old_top, best)
        wide = jnp.concatenate([new_top, new_top], axis=1)
        gained = None
        for s, (_, values, _) in zip(scores, chunks):
            p = jnp.exp2((s - wide) * EXP_SCALE).astype(jnp.bfloat16)
            term = jnp.dot(
                p, jnp.concatenate([values, ones], axis=1), preferred_element_type=jnp.float32
            )
            gained = term if gained is None else gained + term
        if not first:
            fade = jnp.exp2((old_top - new_top) * EXP_SCALE)
            gained = gained + acc[copy] * jnp.concatenate([fade, fade], axis=1)
        acc[copy] = gained
        top[copy] = new_top

    def finish(hd, copy):
        both = acc[copy]
        att[hd, copy, 0, core] = (both[:, :HD] / both[:, HD:]).astype(jnp.bfloat16)

    def ag_up(hd, copy):
        return remote(att.at[hd, copy, 0, core], att.at[hd, copy, 3, core],
                      ag_send.at[hd, copy, 0], ag_recv.at[hd, copy, 2], at_high(h_up, low, core))

    def ag_down(hd, copy):
        return remote(att.at[hd, copy, 0, core], att.at[hd, copy, 1, core],
                      ag_send.at[hd, copy, 1], ag_recv.at[hd, copy, 0], at_high(h_down, low, core))

    def ag_far(hd, copy):
        slot = 3 if copy == 0 else 1
        to = h_up if copy == 0 else h_down
        return remote(att.at[hd, copy, slot, core], att.at[hd, copy, 2, core],
                      ag_send.at[hd, copy, 2], ag_recv.at[hd, copy, 1], at_high(to, low, core))

    def ag_sib(hd, copy, slot):
        return remote(att.at[hd, copy, slot, core], att.at[hd, copy, slot, core],
                      sib_send.at[hd, copy, slot], sib_recv.at[hd, copy, slot], sibling)

    def gather_start(hd, copy):
        ag_up(hd, copy).start()
        ag_down(hd, copy).start()
        ag_sib(hd, copy, 0).start()

    def gather_near(hd):
        for copy in range(2):
            order = (3, 1) if copy == 0 else (1, 3)
            for slot in order:
                if slot == 3:
                    ag_up(hd, copy).wait_recv()
                else:
                    ag_down(hd, copy).wait_recv()
                if slot == order[0]:
                    ag_far(hd, copy).start()
                ag_sib(hd, copy, slot).start()

    def gather_far(hd):
        for copy in range(2):
            ag_far(hd, copy).wait_recv()
            ag_sib(hd, copy, 2).start()

    def own_step(hd):
        keys, values = own(hd, 0)[...], own(hd, 1)[...]
        late_keys = kvbuf[0, 1, :, hd * HD:(hd + 1) * HD]
        late_values = kvbuf[1, 1, :, hd * HD:(hd + 1) * HD]
        attend(hd, 0, [(keys, values, 0)], True)
        attend(hd, 1, [(keys, values, 0), (late_keys, late_values, 9)], True)

    def pair_compute(hd, near, far, copy):
        chunks = [(win[hd, s - 1, 0], win[hd, s - 1, 1], s) for s in (near, far)]
        attend(hd, copy, chunks, False)

    load_q.wait()
    for hd in range(HEADS):
        own_step(hd)
        for step in (1, 2, 3, 4):
            near, far = step, 9 - step
            if step < 4:
                for kv in range(2):
                    kv_copy(hd, near, kv).wait_recv()
                    if step < 3 or kv == 0:
                        kv_copy(hd, near + 1, kv).start()
                    kv_copy(hd, far, kv).wait_recv()
                    kv_copy(hd, far - 1, kv).start()
            else:
                kv_copy(hd, 5, 1).wait_recv()
                kv_copy(hd, 4, 1).start()
                kv_copy(hd, 5, 0).wait_recv()
                if hd == 0:
                    start_kv(1)
                kv_copy(hd, 4, 0).wait_recv()
                kv_copy(hd, 4, 1).wait_recv()
            for copy in range(2):
                pair_compute(hd, near, far, copy)
                if step == 4:
                    finish(hd, copy)
                    gather_start(hd, copy)
            if hd == 0 and step == 4:
                w_stage_1()
            if hd == 1 and step == 2:
                w_stage_2()
            if hd == 1 and step == 3:
                gather_near(0)

    gather_far(0)

    def project(hd, copy, k):
        rows = jnp.concatenate([att[hd, copy, k, 0], att[hd, copy, k, 1]], axis=1)
        weight = panel[k, hd].reshape(2 * HD, FEAT)
        return jnp.dot(rows, weight, preferred_element_type=jnp.float32)

    load_w.wait()
    await_bytes(panel.at[0, :, 1 - core], ws_recv)
    await_bytes(w_half(2, 0), wx_recv.at[2])
    await_bytes(w_half(2, 1), wx_recv.at[3])
    for k in (0, 1, 3, 2):
        for copy in range(2):
            ag_sib(0, copy, k).wait_recv()
            term = project(0, copy, k)
            total[copy] = term if k == 0 else total[copy] + term
    gather_near(1)
    for copy in range(2):
        ag_sib(1, copy, 0).wait_recv()
        total[copy] = total[copy] + project(1, copy, 0)
    for copy in range(2):
        for k in (1, 3):
            ag_sib(1, copy, k).wait_recv()
            total[copy] = total[copy] + project(1, copy, k)
    gather_far(1)
    for copy in range(2):
        ag_sib(1, copy, 2).wait_recv()
        out_ref[copy] = (total[copy] + project(1, copy, 2)).astype(jnp.bfloat16)

    for hd in range(HEADS):
        for slot in range(1, 9):
            for kv in range(2):
                kv_copy(hd, slot, kv).wait_send()
        for copy in range(2):
            ag_up(hd, copy).wait_send()
            ag_down(hd, copy).wait_send()
            ag_far(hd, copy).wait_send()
            for slot in range(4):
                ag_sib(hd, copy, slot).wait_send()
    for copy in w_copies:
        copy.wait_send()
    w_sib.wait_send()
    for copy in wx_copies:
        copy.wait_send()


def on_device(queries, keys_values, block_mask, out_weight):
    weight = out_weight.reshape(HEADS, 2, HD // 2, out_weight.shape[1])
    dma = pltpu.SemaphoreType.DMA
    return pl.pallas_call(
        kernel,
        out_shape=jax.ShapeDtypeStruct((2, TOK, FEAT), jnp.bfloat16),
        in_specs=[
            pl.BlockSpec(memory_space=pltpu.SMEM),
            pl.BlockSpec(memory_space=pl.ANY),
            pl.BlockSpec(memory_space=pl.ANY),
            pl.BlockSpec(memory_space=pl.ANY),
        ],
        out_specs=pl.BlockSpec(memory_space=pltpu.VMEM),
        scratch_shapes=[
            pltpu.VMEM((2, TOK, HEADS * HD), jnp.bfloat16),
            pltpu.VMEM((2, 2, TOK, HEADS * HD), jnp.bfloat16),
            pltpu.VMEM((HEADS, 8, 2, TOK, HD), jnp.bfloat16),
            pltpu.VMEM((2, 10, BLOCKS, 8, TOK), jnp.float32),
            pltpu.VMEM((2, TOK, HD), jnp.float32),
            pltpu.VMEM((2, TOK, 2 * HD), jnp.float32),
            pltpu.VMEM((HEADS, 2, NH, NC, TOK, HD), jnp.bfloat16),
            pltpu.VMEM((NH, HEADS, NC, 2, HD // 2, FEAT), jnp.bfloat16),
            pltpu.VMEM((2, TOK, FEAT), jnp.float32),
            dma((3,)),
            dma((HEADS, 8, 2)),
            dma((HEADS, 8, 2)),
            dma((HEADS, 2, 3)),
            dma((HEADS, 2, 3)),
            dma((HEADS, 2, 4)),
            dma((HEADS, 2, 4)),
            dma((3, NC)),
            dma,
            dma,
            dma,
            dma((4,)),
            dma((4,)),
        ],
        compiler_params=pltpu.CompilerParams(
            collective_id=0, has_side_effects=True, vmem_limit_bytes=40 * 1024 * 1024
        ),
    )(block_mask, queries, keys_values, weight)


def solution(mesh):
    in_specs = (
        P(None, "ctx", "fsdp"),
        P(None, None, "ctx", "fsdp"),
        P("ctx", None),
        P("fsdp", None),
    )
    out_specs = P(None, "ctx", "fsdp")
    return jax.shard_map(
        on_device, mesh=mesh, in_specs=in_specs, out_specs=out_specs, check_vma=False
    )
```

```python
import functools
import math

import jax
import jax.numpy as jnp
from jax import lax
from jax.experimental import pallas as pl
from jax.experimental.pallas import tpu as pltpu
from jax.sharding import PartitionSpec as P

HD = 128
BLK = 64
WINB = 32
NX, NL, NZ, NH, NC = 4, 2, 8, 4, 2
NCTX = NX * NL * NZ
ROW = NZ
TOK = 256
BLOCKS = TOK // BLK
HEADS = 2
FEAT = 512
NEG = -1e30
EXP_SCALE = math.log2(math.e) / math.sqrt(HD)


def mod(value, size):
    return lax.rem(value + 2 * size, size)


def kernel(
    mask_ref, q_hbm, kv_hbm, w_hbm, out_ref,
    qbuf, kvbuf, win, bias, top, acc, att, panel, total,
    local_sem, kv_send, kv_recv, ag_send, ag_recv, sib_send, sib_recv,
    wy_send, wy_recv, ws_send, ws_recv, wx_send, wx_recv,
):
    ctx = lax.axis_index("ctx")
    fsdp = lax.axis_index("fsdp")
    x = ctx // (NL * NZ)
    low = lax.rem(ctx // NZ, NL)
    z = lax.rem(ctx, NZ)
    high = fsdp // NC
    core = lax.rem(fsdp, NC)

    def along(by):
        return (mod(ctx + by, NCTX), fsdp)

    def at_high(h, l, c):
        return ((x * NL + l) * NZ + z, h * NC + c)

    def at_x(by):
        return (mod(x + by, NX) * (NL * NZ) + lax.rem(ctx, NL * NZ), fsdp)

    h_up, h_down, h_far = mod(high + 1, NH), mod(high - 1, NH), mod(high + 2, NH)
    sibling = (ctx, high * NC + (1 - core))

    load_kv = pltpu.make_async_copy(kv_hbm, kvbuf, local_sem.at[0])
    load_q = pltpu.make_async_copy(q_hbm, qbuf, local_sem.at[1])
    load_w = pltpu.make_async_copy(
        w_hbm.at[:, :, :, pl.ds(pl.multiple_of(fsdp * FEAT, FEAT), FEAT)],
        panel.at[0, :, core],
        local_sem.at[2],
    )
    load_kv.start()
    load_q.start()
    load_w.start()

    barrier = pltpu.get_barrier_semaphore()
    sources = [along(-1), along(1), along(-ROW)]
    sources += [at_high(h_up, low, core), at_high(h_down, low, core), sibling]
    for c in range(NC):
        sources += [at_high(h_up, 0, c), at_high(h_down, 1, c), at_high(h_far, 1 - low, c)]
    sources += [at_x(1), at_x(-1)]
    for device in sources:
        pl.semaphore_signal(barrier, inc=1, device_id=device, device_id_type=pl.DeviceIdType.MESH)
    pl.semaphore_wait(barrier, len(sources))

    def remote(src, dst, send, recv, device):
        return pltpu.make_async_remote_copy(
            src_ref=src, dst_ref=dst, send_sem=send, recv_sem=recv,
            device_id=device, device_id_type=pl.DeviceIdType.MESH,
        )

    def own(hd, kv):
        return kvbuf.at[kv, 0, :, hd * HD:(hd + 1) * HD]

    def kv_copy(hd, slot, kv):
        forward = slot < 4 or (slot == 4 and kv == 0)
        if forward:
            src = own(hd, kv) if slot == 1 else win.at[hd, slot - 2, kv]
            device = along(1)
        elif slot == 8:
            src, device = own(hd, kv), along(ROW)
        else:
            src, device = win.at[hd, slot, kv], along(-1)
        return remote(src, win.at[hd, slot - 1, kv], kv_send.at[hd, slot - 1, kv],
                      kv_recv.at[hd, slot - 1, kv], device)

    def start_kv(hd):
        for kv in range(2):
            kv_copy(hd, 1, kv).start()
            kv_copy(hd, 8, kv).start()

    load_kv.wait()

    half, part = x // 2, lax.rem(x, 2)
    sign = 2 * low - 1
    w_targets = [
        (mod(high + sign, NH), 0, mod(-sign, NH)),
        (mod(high + sign, NH), 1, mod(-sign, NH)),
        (h_far, 1 - low, 2),
    ]
    w_copies = []
    for n, (h, l, k) in enumerate(w_targets):
        for c in range(NC):
            cols = pl.ds(pl.multiple_of((h * NC + c) * FEAT, FEAT), FEAT)
            w_copies.append(remote(
                w_hbm.at[half, part, :, cols], panel.at[k, half, core, part],
                wy_send.at[n, c], wy_recv, at_high(h, l, c),
            ))
    other = high * NC + (1 - core)
    w_sib = remote(
        w_hbm.at[:, :, :, pl.ds(pl.multiple_of(other * FEAT, FEAT), FEAT)],
        panel.at[0, :, core], ws_send, ws_recv, sibling,
    )
    w_sib.start()

    def w_stage_0():
        for copy in w_copies:
            copy.start()


    def w_quarter(by):
        xx = mod(x + by, NX)
        return panel.at[1:4, xx // 2, :, lax.rem(xx, 2)]

    def w_half(by, c):
        xx = mod(x + by, NX)
        return panel.at[1:4, xx // 2, c, lax.rem(xx, 2)]

    def await_bytes(ref, sem):
        pltpu.make_async_copy(ref, ref, sem).wait()

    wx_copies = [
        remote(w_quarter(0), w_quarter(0), wx_send.at[0], wx_recv.at[0], at_x(1)),
        remote(w_quarter(0), w_quarter(0), wx_send.at[1], wx_recv.at[1], at_x(-1)),
        remote(w_half(-1, 0), w_half(-1, 0), wx_send.at[2], wx_recv.at[2], at_x(1)),
        remote(w_half(1, 1), w_half(1, 1), wx_send.at[3], wx_recv.at[3], at_x(-1)),
    ]

    def w_stage_1():
        await_bytes(w_quarter(0), wy_recv)
        wx_copies[0].start()
        wx_copies[1].start()

    def w_stage_2():
        await_bytes(w_quarter(-1), wx_recv.at[0])
        wx_copies[2].start()
        await_bytes(w_quarter(1), wx_recv.at[1])
        wx_copies[3].start()

    def attend(hd, copy, chunks, first):
        q = qbuf[copy, :, hd * HD:(hd + 1) * HD]
        scores = []
        for keys, _, slot in chunks:
            s = lax.dot_general(
                q, keys, (((1,), (1,)), ((), ())), preferred_element_type=jnp.float32
            )
            s = s.reshape(BLOCKS, BLK // 8, 8, TOK) + bias[copy, slot][:, None]
            scores.append(s.reshape(TOK, TOK))
        best = scores[0]
        for s in scores[1:]:
            best = jnp.maximum(best, s)
        best = jnp.max(best, axis=1, keepdims=True)
        if first:
            new_top = jnp.broadcast_to(best, (TOK, HD))
        else:
            old_top = top[hd, copy]
            new_top = jnp.maximum(old_top, best)
        wide = jnp.concatenate([new_top, new_top], axis=1)
        gained = None
        for s, (_, values, _) in zip(scores, chunks):
            p = jnp.exp2((s - wide) * EXP_SCALE).astype(jnp.bfloat16)
            term = jnp.dot(
                p, jnp.concatenate([values, ones], axis=1), preferred_element_type=jnp.float32
            )
            gained = term if gained is None else gained + term
        if not first:
            fade = jnp.exp2((old_top - new_top) * EXP_SCALE)
            gained = gained + acc[hd, copy] * jnp.concatenate([fade, fade], axis=1)
        acc[hd, copy] = gained
        top[hd, copy] = new_top

    def finish(hd, copy):
        both = acc[hd, copy]
        att[hd, copy, 0, core] = (both[:, :HD] / both[:, HD:]).astype(jnp.bfloat16)

    def ag_up(hd, copy):
        return remote(att.at[hd, copy, 0, core], att.at[hd, copy, 3, core],
                      ag_send.at[hd, copy, 0], ag_recv.at[hd, copy, 2], at_high(h_up, low, core))

    def ag_down(hd, copy):
        return remote(att.at[hd, copy, 0, core], att.at[hd, copy, 1, core],
                      ag_send.at[hd, copy, 1], ag_recv.at[hd, copy, 0], at_high(h_down, low, core))

    def ag_far(hd, copy):
        slot = 3 if copy == 0 else 1
        to = h_up if copy == 0 else h_down
        return remote(att.at[hd, copy, slot, core], att.at[hd, copy, 2, core],
                      ag_send.at[hd, copy, 2], ag_recv.at[hd, copy, 1], at_high(to, low, core))

    def ag_sib(hd, copy, slot):
        return remote(att.at[hd, copy, slot, core], att.at[hd, copy, slot, core],
                      sib_send.at[hd, copy, slot], sib_recv.at[hd, copy, slot], sibling)

    def gather_start(hd, copy):
        ag_up(hd, copy).start()
        ag_down(hd, copy).start()
        ag_sib(hd, copy, 0).start()

    def gather_near(hd):
        for copy in range(2):
            order = (3, 1) if copy == 0 else (1, 3)
            for slot in order:
                if slot == 3:
                    ag_up(hd, copy).wait_recv()
                else:
                    ag_down(hd, copy).wait_recv()
                if slot == order[0]:
                    ag_far(hd, copy).start()
                ag_sib(hd, copy, slot).start()

    def gather_far(hd):
        for copy in range(2):
            ag_far(hd, copy).wait_recv()
            ag_sib(hd, copy, 2).start()

    def own_step(hd):
        keys, values = own(hd, 0)[...], own(hd, 1)[...]
        late_keys = kvbuf[0, 1, :, hd * HD:(hd + 1) * HD]
        late_values = kvbuf[1, 1, :, hd * HD:(hd + 1) * HD]
        attend(hd, 0, [(keys, values, 0)], True)
        attend(hd, 1, [(keys, values, 0), (late_keys, late_values, 9)], True)

    def pair_compute(hd, near, far, copy):
        chunks = [(win[hd, s - 1, 0], win[hd, s - 1, 1], s) for s in (near, far)]
        attend(hd, copy, chunks, False)

    def kv_step(hd, step):
        for kv in range(2):
            kv_copy(hd, 9 - step, kv).wait_recv()
            if step < 4 or kv == 1:
                kv_copy(hd, 8 - step, kv).start()
        for kv in range(2):
            kv_copy(hd, step, kv).wait_recv()
            if step < 3 or (step == 3 and kv == 0):
                kv_copy(hd, step + 1, kv).start()

    start_kv(0)
    start_kv(1)
    w_stage_0()

    lane_block = lax.broadcasted_iota(jnp.int32, (8, TOK), 1) // BLK
    for slot in range(9):
        here = ctx >= slot
        for a in range(BLOCKS):
            clean = jnp.zeros((8, TOK), jnp.int32)
            noisy = jnp.zeros((8, TOK), jnp.int32)
            for b in range(BLOCKS):
                gap = 4 * slot + a - b
                is_b = lane_block == b
                if 0 <= gap < WINB:
                    clean = jnp.where(is_b, 1, clean)
                if 1 <= gap <= WINB:
                    noisy = jnp.where(is_b, mask_ref[a, gap - 1], noisy)
            present = jnp.where(here, 1, 0)
            bias[0, slot, a] = jnp.where(clean * present == 1, 0.0, NEG)
            bias[1, slot, a] = jnp.where(noisy * present == 1, 0.0, NEG)
    for a in range(BLOCKS):
        bias[1, 9, a] = jnp.where(lane_block == a, 0.0, NEG)

    ones = jnp.ones((TOK, HD), jnp.bfloat16)

    load_q.wait()

    def compute_step(hd, step):
        for copy in range(2):
            pair_compute(hd, step, 9 - step, copy)
            if step == 4:
                finish(hd, copy)
                gather_start(hd, copy)

    def project(hd, copy, spots):
        rows = jnp.concatenate(
            [att[hd, copy, k, c] for k in spots for c in range(NC)], axis=1
        )
        weight = jnp.concatenate(
            [panel[k, hd].reshape(NC * HD, FEAT) for k in spots], axis=0
        )
        return jnp.dot(rows, weight, preferred_element_type=jnp.float32)

    def project_near():
        load_w.wait()
        await_bytes(panel.at[0, :, 1 - core], ws_recv)
        await_bytes(w_half(2, 0), wx_recv.at[2])
        await_bytes(w_half(2, 1), wx_recv.at[3])
        for hd in range(HEADS):
            for copy in range(2):
                for k in (0, 3, 1):
                    ag_sib(hd, copy, k).wait_recv()
                term = project(hd, copy, (0, 3, 1))
                total[copy] = term if hd == 0 else total[copy] + term

    for hd in range(HEADS):
        own_step(hd)
    for step in range(1, 5):
        for hd in range(HEADS):
            kv_step(hd, step)
            compute_step(hd, step)
        if step == 2:
            w_stage_1()
    gather_near(0)
    w_stage_2()
    gather_near(1)
    gather_far(0)
    project_near()
    gather_far(1)
    for copy in range(2):
        for hd in range(HEADS):
            ag_sib(hd, copy, 2).wait_recv()
        rows = jnp.concatenate(
            [att[hd, copy, 2, c] for hd in range(HEADS) for c in range(NC)], axis=1
        )
        weight = panel[2].reshape(HEADS * NC * HD, FEAT)
        term = jnp.dot(rows, weight, preferred_element_type=jnp.float32)
        out_ref[copy] = (total[copy] + term).astype(jnp.bfloat16)

    for hd in range(HEADS):
        for slot in range(1, 9):
            for kv in range(2):
                kv_copy(hd, slot, kv).wait_send()
        for copy in range(2):
            ag_up(hd, copy).wait_send()
            ag_down(hd, copy).wait_send()
            ag_far(hd, copy).wait_send()
            for slot in range(4):
                ag_sib(hd, copy, slot).wait_send()
    for copy in w_copies:
        copy.wait_send()
    w_sib.wait_send()
    for copy in wx_copies:
        copy.wait_send()


def on_device(queries, keys_values, block_mask, out_weight):
    weight = out_weight.reshape(HEADS, 2, HD // 2, out_weight.shape[1])
    dma = pltpu.SemaphoreType.DMA
    return pl.pallas_call(
        kernel,
        out_shape=jax.ShapeDtypeStruct((2, TOK, FEAT), jnp.bfloat16),
        in_specs=[
            pl.BlockSpec(memory_space=pltpu.SMEM),
            pl.BlockSpec(memory_space=pltpu.HBM),
            pl.BlockSpec(memory_space=pltpu.HBM),
            pl.BlockSpec(memory_space=pltpu.HBM),
        ],
        out_specs=pl.BlockSpec(memory_space=pltpu.VMEM),
        scratch_shapes=[
            pltpu.VMEM((2, TOK, HEADS * HD), jnp.bfloat16),
            pltpu.VMEM((2, 2, TOK, HEADS * HD), jnp.bfloat16),
            pltpu.VMEM((HEADS, 8, 2, TOK, HD), jnp.bfloat16),
            pltpu.VMEM((2, 10, BLOCKS, 8, TOK), jnp.float32),
            pltpu.VMEM((HEADS, 2, TOK, HD), jnp.float32),
            pltpu.VMEM((HEADS, 2, TOK, 2 * HD), jnp.float32),
            pltpu.VMEM((HEADS, 2, NH, NC, TOK, HD), jnp.bfloat16),
            pltpu.VMEM((NH, HEADS, NC, 2, HD // 2, FEAT), jnp.bfloat16),
            pltpu.VMEM((2, TOK, FEAT), jnp.float32),
            dma((3,)),
            dma((HEADS, 8, 2)),
            dma((HEADS, 8, 2)),
            dma((HEADS, 2, 3)),
            dma((HEADS, 2, 3)),
            dma((HEADS, 2, 4)),
            dma((HEADS, 2, 4)),
            dma((3, NC)),
            dma,
            dma,
            dma,
            dma((4,)),
            dma((4,)),
        ],
        compiler_params=pltpu.CompilerParams(
            collective_id=0, has_side_effects=True, vmem_limit_bytes=62 * 1024 * 1024
        ),
    )(block_mask, queries, keys_values, weight)


def solution(mesh):
    in_specs = (
        P(None, "ctx", "fsdp"),
        P(None, None, "ctx", "fsdp"),
        P("ctx", None),
        P("fsdp", None),
    )
    out_specs = P(None, "ctx", "fsdp")
    return jax.shard_map(
        on_device, mesh=mesh, in_specs=in_specs, out_specs=out_specs, check_vma=False
    )
```

```python
import functools
import math

import jax
import jax.numpy as jnp
from jax import lax
from jax.experimental import pallas as pl
from jax.experimental.pallas import tpu as pltpu
from jax.sharding import PartitionSpec as P

HD = 128
BLK = 64
WINB = 32
NX, NL, NZ, NH, NC = 4, 2, 8, 4, 2
NCTX = NX * NL * NZ
ROW = NZ
TOK = 256
BLOCKS = TOK // BLK
HEADS = 2
FEAT = 512
NEG = -1e30
PAIR_STEP, RING_STEP = 1, 2
EXP_SCALE = math.log2(math.e) / math.sqrt(HD)


def mod(value, size):
    return lax.rem(value + 2 * size, size)


def kernel(
    mask_ref, q_hbm, kv_hbm, w_hbm, out_ref,
    qbuf, kvbuf, win, bias, top, acc, att, panel, total,
    local_sem, kv_send, kv_recv, ag_send, ag_recv, sib_send, sib_recv,
    wy_send, wy_recv, wp_send, wp_recv, ws_send, ws_recv, wx_send, wx_recv,
):
    ctx = lax.axis_index("ctx")
    fsdp = lax.axis_index("fsdp")
    x = ctx // (NL * NZ)
    low = lax.rem(ctx // NZ, NL)
    z = lax.rem(ctx, NZ)
    high = fsdp // NC
    core = lax.rem(fsdp, NC)

    def along(by):
        return (mod(ctx + by, NCTX), fsdp)

    def at_high(h, l, c):
        return ((x * NL + l) * NZ + z, h * NC + c)

    def at_x(by):
        return (mod(x + by, NX) * (NL * NZ) + lax.rem(ctx, NL * NZ), fsdp)

    h_up, h_down, h_far = mod(high + 1, NH), mod(high - 1, NH), mod(high + 2, NH)
    sibling = (ctx, high * NC + (1 - core))

    load_kv = pltpu.make_async_copy(kv_hbm, kvbuf, local_sem.at[0])
    load_q = pltpu.make_async_copy(q_hbm, qbuf, local_sem.at[1])
    load_w = pltpu.make_async_copy(
        w_hbm.at[:, :, :, :, pl.ds(pl.multiple_of(fsdp * FEAT, FEAT), FEAT)],
        panel.at[0, :, core],
        local_sem.at[2],
    )
    load_kv.start()
    load_q.start()
    load_w.start()

    barrier = pltpu.get_barrier_semaphore()
    sources = [along(-1), along(1), along(-ROW)]
    sources += [at_high(h_up, low, core), at_high(h_down, low, core), sibling]
    for c in range(NC):
        sources += [at_high(h_up, 0, c), at_high(h_down, 1, c), at_high(h_far, 1 - low, c)]
    sources += [at_x(1), at_x(-1)]
    for device in sources:
        pl.semaphore_signal(barrier, inc=1, device_id=device, device_id_type=pl.DeviceIdType.MESH)
    pl.semaphore_wait(barrier, len(sources))

    def remote(src, dst, send, recv, device):
        return pltpu.make_async_remote_copy(
            src_ref=src, dst_ref=dst, send_sem=send, recv_sem=recv,
            device_id=device, device_id_type=pl.DeviceIdType.MESH,
        )

    def own(hd, kv):
        return kvbuf.at[kv, 0, :, hd * HD:(hd + 1) * HD]

    def kv_copy(hd, slot, kv):
        forward = slot < 4 or (slot == 4 and kv == 0)
        if forward:
            src = own(hd, kv) if slot == 1 else win.at[hd, slot - 2, kv]
            device = along(1)
        elif slot == 8:
            src, device = own(hd, kv), along(ROW)
        else:
            src, device = win.at[hd, slot, kv], along(-1)
        return remote(src, win.at[hd, slot - 1, kv], kv_send.at[hd, slot - 1, kv],
                      kv_recv.at[hd, slot - 1, kv], device)

    def start_kv(hd):
        for kv in range(2):
            kv_copy(hd, 1, kv).start()
            kv_copy(hd, 8, kv).start()

    load_kv.wait()

    half, part, odd = x // 2, lax.rem(x, 2), lax.rem(z, 2)
    sign = 2 * low - 1
    w_targets = [
        (mod(high + sign, NH), 0, mod(-sign, NH)),
        (mod(high + sign, NH), 1, mod(-sign, NH)),
        (h_far, 1 - low, 2),
    ]
    w_copies = []
    for n, (h, l, k) in enumerate(w_targets):
        for c in range(NC):
            cols = pl.ds(pl.multiple_of((h * NC + c) * FEAT, FEAT), FEAT)
            w_copies.append(remote(
                w_hbm.at[half, part, odd, :, cols], panel.at[k, half, core, part, odd],
                wy_send.at[n, c], wy_recv, at_high(h, l, c),
            ))
    other = high * NC + (1 - core)
    w_sib = remote(
        w_hbm.at[:, :, :, :, pl.ds(pl.multiple_of(other * FEAT, FEAT), FEAT)],
        panel.at[0, :, core], ws_send, ws_recv, sibling,
    )
    w_sib.start()

    def w_stage_0():
        for copy in w_copies:
            copy.start()


    def w_quarter(by):
        xx = mod(x + by, NX)
        return panel.at[1:4, xx // 2, :, lax.rem(xx, 2)]

    def w_half(by, c):
        xx = mod(x + by, NX)
        return panel.at[1:4, xx // 2, c, lax.rem(xx, 2)]

    def await_bytes(ref, sem):
        pltpu.make_async_copy(ref, ref, sem).wait()

    wx_copies = [
        remote(w_quarter(0), w_quarter(0), wx_send.at[0], wx_recv.at[0], at_x(1)),
        remote(w_quarter(0), w_quarter(0), wx_send.at[1], wx_recv.at[1], at_x(-1)),
        remote(w_half(-1, 0), w_half(-1, 0), wx_send.at[2], wx_recv.at[2], at_x(1)),
        remote(w_half(1, 1), w_half(1, 1), wx_send.at[3], wx_recv.at[3], at_x(-1)),
    ]

    share = panel.at[1:4, half, :, part, odd]
    w_pair = remote(share, share, wp_send, wp_recv, along(1 - 2 * odd))

    def w_stage_1():
        await_bytes(share, wy_recv)
        w_pair.start()

    def w_stage_2():
        w_pair.wait_recv()
        wx_copies[0].start()
        wx_copies[1].start()

    def w_stage_3():
        await_bytes(w_quarter(-1), wx_recv.at[0])
        wx_copies[2].start()
        await_bytes(w_quarter(1), wx_recv.at[1])
        wx_copies[3].start()

    def attend(hd, copy, chunks, first):
        q = qbuf[copy, :, hd * HD:(hd + 1) * HD]
        scores = []
        for keys, _, slot in chunks:
            s = lax.dot_general(
                q, keys, (((1,), (1,)), ((), ())), preferred_element_type=jnp.float32
            )
            s = s.reshape(BLOCKS, BLK // 8, 8, TOK) + bias[copy, slot][:, None]
            scores.append(s.reshape(TOK, TOK))
        best = scores[0]
        for s in scores[1:]:
            best = jnp.maximum(best, s)
        best = jnp.max(best, axis=1, keepdims=True)
        if first:
            new_top = jnp.broadcast_to(best, (TOK, HD))
        else:
            old_top = top[hd, copy]
            new_top = jnp.maximum(old_top, best)
        wide = jnp.concatenate([new_top, new_top], axis=1)
        gained = None
        for s, (_, values, _) in zip(scores, chunks):
            p = jnp.exp2((s - wide) * EXP_SCALE).astype(jnp.bfloat16)
            term = jnp.dot(
                p, jnp.concatenate([values, ones], axis=1), preferred_element_type=jnp.float32
            )
            gained = term if gained is None else gained + term
        if not first:
            fade = jnp.exp2((old_top - new_top) * EXP_SCALE)
            gained = gained + acc[hd, copy] * jnp.concatenate([fade, fade], axis=1)
        acc[hd, copy] = gained
        top[hd, copy] = new_top

    def finish(hd, copy):
        both = acc[hd, copy]
        att[hd, copy, 0, core] = (both[:, :HD] / both[:, HD:]).astype(jnp.bfloat16)

    def ag_up(hd, copy):
        return remote(att.at[hd, copy, 0, core], att.at[hd, copy, 3, core],
                      ag_send.at[hd, copy, 0], ag_recv.at[hd, copy, 2], at_high(h_up, low, core))

    def ag_down(hd, copy):
        return remote(att.at[hd, copy, 0, core], att.at[hd, copy, 1, core],
                      ag_send.at[hd, copy, 1], ag_recv.at[hd, copy, 0], at_high(h_down, low, core))

    def ag_far(hd, copy):
        slot = 3 if copy == 0 else 1
        to = h_up if copy == 0 else h_down
        return remote(att.at[hd, copy, slot, core], att.at[hd, copy, 2, core],
                      ag_send.at[hd, copy, 2], ag_recv.at[hd, copy, 1], at_high(to, low, core))

    def ag_sib(hd, copy, slot):
        return remote(att.at[hd, copy, slot, core], att.at[hd, copy, slot, core],
                      sib_send.at[hd, copy, slot], sib_recv.at[hd, copy, slot], sibling)

    def gather_start(hd, copy):
        ag_up(hd, copy).start()
        ag_down(hd, copy).start()
        ag_sib(hd, copy, 0).start()

    def gather_near(hd):
        for copy in range(2):
            order = (3, 1) if copy == 0 else (1, 3)
            for slot in order:
                if slot == 3:
                    ag_up(hd, copy).wait_recv()
                else:
                    ag_down(hd, copy).wait_recv()
                if slot == order[0]:
                    ag_far(hd, copy).start()
                ag_sib(hd, copy, slot).start()

    def gather_far(hd):
        for copy in range(2):
            ag_far(hd, copy).wait_recv()
            ag_sib(hd, copy, 2).start()

    def own_step(hd):
        keys, values = own(hd, 0)[...], own(hd, 1)[...]
        late_keys = kvbuf[0, 1, :, hd * HD:(hd + 1) * HD]
        late_values = kvbuf[1, 1, :, hd * HD:(hd + 1) * HD]
        attend(hd, 0, [(keys, values, 0)], True)
        attend(hd, 1, [(keys, values, 0), (late_keys, late_values, 9)], True)

    def pair_compute(hd, near, far, copy):
        chunks = [(win[hd, s - 1, 0], win[hd, s - 1, 1], s) for s in (near, far)]
        attend(hd, copy, chunks, False)

    def kv_step(hd, step):
        for kv in range(2):
            kv_copy(hd, 9 - step, kv).wait_recv()
            if step < 4 or kv == 1:
                kv_copy(hd, 8 - step, kv).start()
        for kv in range(2):
            kv_copy(hd, step, kv).wait_recv()
            if step < 3 or (step == 3 and kv == 0):
                kv_copy(hd, step + 1, kv).start()

    start_kv(0)
    start_kv(1)
    w_stage_0()

    lane_block = lax.broadcasted_iota(jnp.int32, (8, TOK), 1) // BLK
    for slot in range(9):
        here = ctx >= slot
        for a in range(BLOCKS):
            clean = jnp.zeros((8, TOK), jnp.int32)
            noisy = jnp.zeros((8, TOK), jnp.int32)
            for b in range(BLOCKS):
                gap = 4 * slot + a - b
                is_b = lane_block == b
                if 0 <= gap < WINB:
                    clean = jnp.where(is_b, 1, clean)
                if 1 <= gap <= WINB:
                    noisy = jnp.where(is_b, mask_ref[a, gap - 1], noisy)
            present = jnp.where(here, 1, 0)
            bias[0, slot, a] = jnp.where(clean * present == 1, 0.0, NEG)
            bias[1, slot, a] = jnp.where(noisy * present == 1, 0.0, NEG)
    for a in range(BLOCKS):
        bias[1, 9, a] = jnp.where(lane_block == a, 0.0, NEG)

    ones = jnp.ones((TOK, HD), jnp.bfloat16)

    load_q.wait()

    def compute_step(hd, step):
        for copy in range(2):
            pair_compute(hd, step, 9 - step, copy)
            if step == 4:
                finish(hd, copy)
                gather_start(hd, copy)

    def project(hd, copy, spots):
        rows = jnp.concatenate(
            [att[hd, copy, k, c] for k in spots for c in range(NC)], axis=1
        )
        weight = jnp.concatenate(
            [panel[k, hd].reshape(NC * HD, FEAT) for k in spots], axis=0
        )
        return jnp.dot(rows, weight, preferred_element_type=jnp.float32)

    def project_near():
        load_w.wait()
        await_bytes(panel.at[0, :, 1 - core], ws_recv)
        await_bytes(w_half(2, 0), wx_recv.at[2])
        await_bytes(w_half(2, 1), wx_recv.at[3])
        for hd in range(HEADS):
            for copy in range(2):
                for k in (0, 3, 1):
                    ag_sib(hd, copy, k).wait_recv()
                term = project(hd, copy, (0, 3, 1))
                total[copy] = term if hd == 0 else total[copy] + term

    for hd in range(HEADS):
        own_step(hd)
    for step in range(1, 5):
        for hd in range(HEADS):
            kv_step(hd, step)
            compute_step(hd, step)
        if step == PAIR_STEP:
            w_stage_1()
        if step == RING_STEP:
            w_stage_2()
    gather_near(0)
    w_stage_3()
    gather_near(1)
    gather_far(0)
    project_near()
    gather_far(1)
    for copy in range(2):
        for hd in range(HEADS):
            ag_sib(hd, copy, 2).wait_recv()
        rows = jnp.concatenate(
            [att[hd, copy, 2, c] for hd in range(HEADS) for c in range(NC)], axis=1
        )
        weight = panel[2].reshape(HEADS * NC * HD, FEAT)
        term = jnp.dot(rows, weight, preferred_element_type=jnp.float32)
        out_ref[copy] = (total[copy] + term).astype(jnp.bfloat16)

    for hd in range(HEADS):
        for slot in range(1, 9):
            for kv in range(2):
                kv_copy(hd, slot, kv).wait_send()
        for copy in range(2):
            ag_up(hd, copy).wait_send()
            ag_down(hd, copy).wait_send()
            ag_far(hd, copy).wait_send()
            for slot in range(4):
                ag_sib(hd, copy, slot).wait_send()
    for copy in w_copies:
        copy.wait_send()
    w_sib.wait_send()
    w_pair.wait_send()
    for copy in wx_copies:
        copy.wait_send()


def on_device(queries, keys_values, block_mask, out_weight):
    weight = out_weight.reshape(HEADS, 2, 2, HD // 4, out_weight.shape[1])
    dma = pltpu.SemaphoreType.DMA
    return pl.pallas_call(
        kernel,
        out_shape=jax.ShapeDtypeStruct((2, TOK, FEAT), jnp.bfloat16),
        in_specs=[
            pl.BlockSpec(memory_space=pltpu.SMEM),
            pl.BlockSpec(memory_space=pltpu.HBM),
            pl.BlockSpec(memory_space=pltpu.HBM),
            pl.BlockSpec(memory_space=pltpu.HBM),
        ],
        out_specs=pl.BlockSpec(memory_space=pltpu.VMEM),
        scratch_shapes=[
            pltpu.VMEM((2, TOK, HEADS * HD), jnp.bfloat16),
            pltpu.VMEM((2, 2, TOK, HEADS * HD), jnp.bfloat16),
            pltpu.VMEM((HEADS, 8, 2, TOK, HD), jnp.bfloat16),
            pltpu.VMEM((2, 10, BLOCKS, 8, TOK), jnp.float32),
            pltpu.VMEM((HEADS, 2, TOK, HD), jnp.float32),
            pltpu.VMEM((HEADS, 2, TOK, 2 * HD), jnp.float32),
            pltpu.VMEM((HEADS, 2, NH, NC, TOK, HD), jnp.bfloat16),
            pltpu.VMEM((NH, HEADS, NC, 2, 2, HD // 4, FEAT), jnp.bfloat16),
            pltpu.VMEM((2, TOK, FEAT), jnp.float32),
            dma((3,)),
            dma((HEADS, 8, 2)),
            dma((HEADS, 8, 2)),
            dma((HEADS, 2, 3)),
            dma((HEADS, 2, 3)),
            dma((HEADS, 2, 4)),
            dma((HEADS, 2, 4)),
            dma((3, NC)),
            dma,
            dma,
            dma,
            dma,
            dma,
            dma((4,)),
            dma((4,)),
        ],
        compiler_params=pltpu.CompilerParams(
            collective_id=0, has_side_effects=True, vmem_limit_bytes=62 * 1024 * 1024
        ),
    )(block_mask, queries, keys_values, weight)


def solution(mesh):
    in_specs = (
        P(None, "ctx", "fsdp"),
        P(None, None, "ctx", "fsdp"),
        P("ctx", None),
        P("fsdp", None),
    )
    out_specs = P(None, "ctx", "fsdp")
    return jax.shard_map(
        on_device, mesh=mesh, in_specs=in_specs, out_specs=out_specs, check_vma=False
    )
```

```python
import functools
import math

import jax
import jax.numpy as jnp
from jax import lax
from jax.experimental import pallas as pl
from jax.experimental.pallas import tpu as pltpu
from jax.sharding import PartitionSpec as P

HD = 128
BLK = 64
WINB = 32
NX, NL, NZ, NH, NC = 4, 2, 8, 4, 2
NCTX = NX * NL * NZ
ROW = NZ
TOK = 256
BLOCKS = TOK // BLK
HEADS = 2
FEAT = 512
NEG = -1e30
PAIR_STEP, RING_STEP = 1, 2
EXP_SCALE = math.log2(math.e) / math.sqrt(HD)


def mod(value, size):
    return lax.rem(value + 2 * size, size)


def kernel(
    mask_ref, q_hbm, kv_hbm, w_hbm, out_ref,
    qbuf, kvbuf, win, bias, top, acc, att, panel, total,
    local_sem, kv_send, kv_recv, ag_send, ag_recv, sib_send, sib_recv,
    wy_send, wy_recv, wp_send, wp_recv, ws_send, ws_recv, wx_send, wx_recv,
):
    ctx = lax.axis_index("ctx")
    fsdp = lax.axis_index("fsdp")
    x = ctx // (NL * NZ)
    low = lax.rem(ctx // NZ, NL)
    z = lax.rem(ctx, NZ)
    high = fsdp // NC
    core = lax.rem(fsdp, NC)

    def along(by):
        return (mod(ctx + by, NCTX), fsdp)

    def at_high(h, l, c):
        return ((x * NL + l) * NZ + z, h * NC + c)

    def at_x(by):
        return (mod(x + by, NX) * (NL * NZ) + lax.rem(ctx, NL * NZ), fsdp)

    h_up, h_down, h_far = mod(high + 1, NH), mod(high - 1, NH), mod(high + 2, NH)
    sibling = (ctx, high * NC + (1 - core))

    load_kv = pltpu.make_async_copy(kv_hbm, kvbuf, local_sem.at[0])
    load_q = pltpu.make_async_copy(q_hbm, qbuf, local_sem.at[1])
    load_w = pltpu.make_async_copy(
        w_hbm.at[:, :, :, :, pl.ds(pl.multiple_of(fsdp * FEAT, FEAT), FEAT)],
        panel.at[0, :, core],
        local_sem.at[2],
    )
    load_kv.start()
    load_q.start()
    load_w.start()

    barrier = pltpu.get_barrier_semaphore()
    sources = [along(-1), along(1), along(-ROW)]
    sources += [at_high(h_up, low, core), at_high(h_down, low, core), sibling]
    for c in range(NC):
        sources += [at_high(h_up, 0, c), at_high(h_down, 1, c), at_high(h_far, 1 - low, c)]
    sources += [at_x(1), at_x(-1)]
    for device in sources:
        pl.semaphore_signal(barrier, inc=1, device_id=device, device_id_type=pl.DeviceIdType.MESH)
    pl.semaphore_wait(barrier, len(sources))

    def remote(src, dst, send, recv, device):
        return pltpu.make_async_remote_copy(
            src_ref=src, dst_ref=dst, send_sem=send, recv_sem=recv,
            device_id=device, device_id_type=pl.DeviceIdType.MESH,
        )

    def own(hd, kv):
        return kvbuf.at[kv, 0, :, hd * HD:(hd + 1) * HD]

    def kv_copy(hd, slot, kv):
        forward = slot < 4 or (slot == 4 and kv == 0)
        if forward:
            src = own(hd, kv) if slot == 1 else win.at[hd, slot - 2, kv]
            device = along(1)
        elif slot == 8:
            src, device = own(hd, kv), along(ROW)
        else:
            src, device = win.at[hd, slot, kv], along(-1)
        return remote(src, win.at[hd, slot - 1, kv], kv_send.at[hd, slot - 1, kv],
                      kv_recv.at[hd, slot - 1, kv], device)

    def start_kv(hd):
        for kv in range(2):
            kv_copy(hd, 1, kv).start()
            kv_copy(hd, 8, kv).start()

    load_kv.wait()

    half, part, odd = x // 2, lax.rem(x, 2), lax.rem(z, 2)
    sign = 2 * low - 1
    w_targets = [
        (mod(high + sign, NH), 0, mod(-sign, NH)),
        (mod(high + sign, NH), 1, mod(-sign, NH)),
        (h_far, 1 - low, 2),
    ]
    w_copies = []
    for n, (h, l, k) in enumerate(w_targets):
        for c in range(NC):
            cols = pl.ds(pl.multiple_of((h * NC + c) * FEAT, FEAT), FEAT)
            w_copies.append(remote(
                w_hbm.at[half, part, odd, :, cols], panel.at[k, half, core, part, odd],
                wy_send.at[n, c], wy_recv, at_high(h, l, c),
            ))
    other = high * NC + (1 - core)
    w_sib = remote(
        w_hbm.at[:, :, :, :, pl.ds(pl.multiple_of(other * FEAT, FEAT), FEAT)],
        panel.at[0, :, core], ws_send, ws_recv, sibling,
    )
    w_sib.start()

    def w_stage_0():
        for copy in w_copies:
            copy.start()

    def w_quarter(by):
        xx = mod(x + by, NX)
        return panel.at[1:4, xx // 2, :, lax.rem(xx, 2)]

    def w_half(by, c):
        xx = mod(x + by, NX)
        return panel.at[1:4, xx // 2, c, lax.rem(xx, 2)]

    def await_bytes(ref, sem):
        pltpu.make_async_copy(ref, ref, sem).wait()

    wx_copies = [
        remote(w_quarter(0), w_quarter(0), wx_send.at[0], wx_recv.at[0], at_x(1)),
        remote(w_quarter(0), w_quarter(0), wx_send.at[1], wx_recv.at[1], at_x(-1)),
        remote(w_half(-1, 0), w_half(-1, 0), wx_send.at[2], wx_recv.at[2], at_x(1)),
        remote(w_half(1, 1), w_half(1, 1), wx_send.at[3], wx_recv.at[3], at_x(-1)),
    ]

    share = panel.at[1:4, half, :, part, odd]
    w_pair = remote(share, share, wp_send, wp_recv, along(1 - 2 * odd))

    def w_stage_1():
        await_bytes(share, wy_recv)
        w_pair.start()

    def w_stage_2():
        w_pair.wait_recv()
        wx_copies[0].start()
        wx_copies[1].start()

    def w_stage_3():
        await_bytes(w_quarter(-1), wx_recv.at[0])
        wx_copies[2].start()
        await_bytes(w_quarter(1), wx_recv.at[1])
        wx_copies[3].start()

    def attend(hd, copy, chunks, first):
        q = qbuf[copy, :, hd * HD:(hd + 1) * HD]
        scores = []
        for keys, _, slot in chunks:
            s = lax.dot_general(
                q, keys, (((1,), (1,)), ((), ())), preferred_element_type=jnp.float32
            )
            s = s.reshape(BLOCKS, BLK // 8, 8, TOK) + bias[copy, slot][:, None]
            scores.append(s.reshape(TOK, TOK))
        best = scores[0]
        for s in scores[1:]:
            best = jnp.maximum(best, s)
        best = jnp.max(best, axis=1, keepdims=True)
        if first:
            new_top = jnp.broadcast_to(best, (TOK, HD))
        else:
            old_top = top[hd, copy]
            new_top = jnp.maximum(old_top, best)
        wide = jnp.concatenate([new_top, new_top], axis=1)
        gained = None
        for s, (_, values, _) in zip(scores, chunks):
            p = jnp.exp2((s - wide) * EXP_SCALE).astype(jnp.bfloat16)
            term = jnp.dot(
                p, jnp.concatenate([values, ones], axis=1), preferred_element_type=jnp.float32
            )
            gained = term if gained is None else gained + term
        if not first:
            fade = jnp.exp2((old_top - new_top) * EXP_SCALE)
            gained = gained + acc[hd, copy] * jnp.concatenate([fade, fade], axis=1)
        acc[hd, copy] = gained
        top[hd, copy] = new_top

    def finish(hd, copy):
        both = acc[hd, copy]
        att[hd, copy, 0, core] = (both[:, :HD] / both[:, HD:]).astype(jnp.bfloat16)

    def ag_up(hd, copy):
        return remote(att.at[hd, copy, 0, core], att.at[hd, copy, 3, core],
                      ag_send.at[hd, copy, 0], ag_recv.at[hd, copy, 2], at_high(h_up, low, core))

    def ag_down(hd, copy):
        return remote(att.at[hd, copy, 0, core], att.at[hd, copy, 1, core],
                      ag_send.at[hd, copy, 1], ag_recv.at[hd, copy, 0], at_high(h_down, low, core))

    def ag_far(hd, copy):
        slot = 3 if copy == 0 else 1
        to = h_up if copy == 0 else h_down
        return remote(att.at[hd, copy, slot, core], att.at[hd, copy, 2, core],
                      ag_send.at[hd, copy, 2], ag_recv.at[hd, copy, 1], at_high(to, low, core))

    def ag_sib(hd, copy, slot):
        return remote(att.at[hd, copy, slot, core], att.at[hd, copy, slot, core],
                      sib_send.at[hd, copy, slot], sib_recv.at[hd, copy, slot], sibling)

    def gather_start(hd, copy):
        ag_up(hd, copy).start()
        ag_down(hd, copy).start()
        ag_sib(hd, copy, 0).start()

    def gather_near(hd):
        for copy in range(2):
            order = (3, 1) if copy == 0 else (1, 3)
            for slot in order:
                if slot == 3:
                    ag_up(hd, copy).wait_recv()
                else:
                    ag_down(hd, copy).wait_recv()
                if slot == order[0]:
                    ag_far(hd, copy).start()
                ag_sib(hd, copy, slot).start()

    def gather_far(hd):
        for copy in range(2):
            ag_far(hd, copy).wait_recv()
            ag_sib(hd, copy, 2).start()

    def own_step(hd):
        keys, values = own(hd, 0)[...], own(hd, 1)[...]
        late_keys = kvbuf[0, 1, :, hd * HD:(hd + 1) * HD]
        late_values = kvbuf[1, 1, :, hd * HD:(hd + 1) * HD]
        attend(hd, 0, [(keys, values, 0)], True)
        attend(hd, 1, [(keys, values, 0), (late_keys, late_values, 9)], True)

    def pair_compute(hd, near, far, copy):
        chunks = [(win[hd, s - 1, 0], win[hd, s - 1, 1], s) for s in (near, far)]
        attend(hd, copy, chunks, False)

    def kv_step(hd, step):
        for kv in range(2):
            kv_copy(hd, 9 - step, kv).wait_recv()
            if step < 4 or kv == 1:
                kv_copy(hd, 8 - step, kv).start()
        for kv in range(2):
            kv_copy(hd, step, kv).wait_recv()
            if step < 3 or (step == 3 and kv == 0):
                kv_copy(hd, step + 1, kv).start()

    start_kv(0)
    start_kv(1)
    w_stage_0()

    lane_block = lax.broadcasted_iota(jnp.int32, (8, TOK), 1) // BLK
    for slot in range(9):
        here = ctx >= slot
        for a in range(BLOCKS):
            clean = jnp.zeros((8, TOK), jnp.int32)
            noisy = jnp.zeros((8, TOK), jnp.int32)
            for b in range(BLOCKS):
                gap = 4 * slot + a - b
                is_b = lane_block == b
                if 0 <= gap < WINB:
                    clean = jnp.where(is_b, 1, clean)
                if 1 <= gap <= WINB:
                    noisy = jnp.where(is_b, mask_ref[a, gap - 1], noisy)
            present = jnp.where(here, 1, 0)
            bias[0, slot, a] = jnp.where(clean * present == 1, 0.0, NEG)
            bias[1, slot, a] = jnp.where(noisy * present == 1, 0.0, NEG)
    for a in range(BLOCKS):
        bias[1, 9, a] = jnp.where(lane_block == a, 0.0, NEG)

    ones = jnp.ones((TOK, HD), jnp.bfloat16)

    load_q.wait()

    def compute_step(hd, step):
        for copy in range(2):
            pair_compute(hd, step, 9 - step, copy)
            if step == 4:
                finish(hd, copy)
                gather_start(hd, copy)

    def project(hd, copy, spots):
        rows = jnp.concatenate(
            [att[hd, copy, k, c] for k in spots for c in range(NC)], axis=1
        )
        weight = jnp.concatenate(
            [panel[k, hd].reshape(NC * HD, FEAT) for k in spots], axis=0
        )
        return jnp.dot(rows, weight, preferred_element_type=jnp.float32)

    def project_near():
        load_w.wait()
        await_bytes(panel.at[0, :, 1 - core], ws_recv)
        await_bytes(w_half(2, 0), wx_recv.at[2])
        await_bytes(w_half(2, 1), wx_recv.at[3])
        for hd in range(HEADS):
            for copy in range(2):
                for k in (0, 3, 1):
                    ag_sib(hd, copy, k).wait_recv()
                term = project(hd, copy, (0, 3, 1))
                total[copy] = term if hd == 0 else total[copy] + term

    for hd in range(HEADS):
        own_step(hd)
    for step in range(1, 5):
        for hd in range(HEADS):
            kv_step(hd, step)
            if step == 4:
                compute_step(hd, step)
        if step < 4:
            for hd in range(HEADS):
                compute_step(hd, step)
        if step == PAIR_STEP:
            w_stage_1()
        if step == RING_STEP:
            w_stage_2()
    gather_near(0)
    w_stage_3()
    gather_near(1)
    gather_far(0)
    project_near()

    for hd in range(HEADS):
        for slot in range(1, 9):
            for kv in range(2):
                kv_copy(hd, slot, kv).wait_send()
        for copy in range(2):
            ag_up(hd, copy).wait_send()
            ag_down(hd, copy).wait_send()
            for slot in (0, 1, 3):
                ag_sib(hd, copy, slot).wait_send()
            if hd == 0:
                ag_far(hd, copy).wait_send()
                ag_sib(hd, copy, 2).wait_send()
    for copy in w_copies + wx_copies + [w_sib, w_pair]:
        copy.wait_send()

    gather_far(1)
    for copy in range(2):
        for hd in range(HEADS):
            ag_sib(hd, copy, 2).wait_recv()
        rows = jnp.concatenate(
            [att[hd, copy, 2, c] for hd in range(HEADS) for c in range(NC)], axis=1
        )
        weight = panel[2].reshape(HEADS * NC * HD, FEAT)
        term = jnp.dot(rows, weight, preferred_element_type=jnp.float32)
        out_ref[copy] = (total[copy] + term).astype(jnp.bfloat16)

    for copy in range(2):
        ag_far(1, copy).wait_send()
        ag_sib(1, copy, 2).wait_send()


def on_device(queries, keys_values, block_mask, out_weight):
    weight = out_weight.reshape(HEADS, 2, 2, HD // 4, out_weight.shape[1])
    dma = pltpu.SemaphoreType.DMA
    return pl.pallas_call(
        kernel,
        out_shape=jax.ShapeDtypeStruct((2, TOK, FEAT), jnp.bfloat16),
        in_specs=[
            pl.BlockSpec(memory_space=pltpu.SMEM),
            pl.BlockSpec(memory_space=pltpu.HBM),
            pl.BlockSpec(memory_space=pltpu.HBM),
            pl.BlockSpec(memory_space=pltpu.HBM),
        ],
        out_specs=pl.BlockSpec(memory_space=pltpu.VMEM),
        scratch_shapes=[
            pltpu.VMEM((2, TOK, HEADS * HD), jnp.bfloat16),
            pltpu.VMEM((2, 2, TOK, HEADS * HD), jnp.bfloat16),
            pltpu.VMEM((HEADS, 8, 2, TOK, HD), jnp.bfloat16),
            pltpu.VMEM((2, 10, BLOCKS, 8, TOK), jnp.float32),
            pltpu.VMEM((HEADS, 2, TOK, HD), jnp.float32),
            pltpu.VMEM((HEADS, 2, TOK, 2 * HD), jnp.float32),
            pltpu.VMEM((HEADS, 2, NH, NC, TOK, HD), jnp.bfloat16),
            pltpu.VMEM((NH, HEADS, NC, 2, 2, HD // 4, FEAT), jnp.bfloat16),
            pltpu.VMEM((2, TOK, FEAT), jnp.float32),
            dma((3,)),
            dma((HEADS, 8, 2)),
            dma((HEADS, 8, 2)),
            dma((HEADS, 2, 3)),
            dma((HEADS, 2, 3)),
            dma((HEADS, 2, 4)),
            dma((HEADS, 2, 4)),
            dma((3, NC)),
            dma,
            dma,
            dma,
            dma,
            dma,
            dma((4,)),
            dma((4,)),
        ],
        compiler_params=pltpu.CompilerParams(
            collective_id=0, has_side_effects=True, vmem_limit_bytes=62 * 1024 * 1024
        ),
    )(block_mask, queries, keys_values, weight)


def solution(mesh):
    in_specs = (
        P(None, "ctx", "fsdp"),
        P(None, None, "ctx", "fsdp"),
        P("ctx", None),
        P("fsdp", None),
    )
    out_specs = P(None, "ctx", "fsdp")
    return jax.shard_map(
        on_device, mesh=mesh, in_specs=in_specs, out_specs=out_specs, check_vma=False
    )
```
